512 devices in a mesh: feed: 32 (over x, z), chan: 8 (over y), tm: 2 (over core).
Axes of the slice: x: 4, y: 8, z: 8, core: 2. Of those that a mesh axis runs over, the one named last changes fastest.
Arguments:
- voltages: bfloat16 [2, 512, 32, 2, 4096], P(None, 'tm', 'chan', None, 'feed'), may hold values from -6 to 6
- beam_refs: bfloat16 [2, 2, 32, 8, 32, 2, 32, 512], P(None, 'tm', 'feed', None, 'chan'), may hold values from -3 to 3
- beam_weight: float32 [32, 512], replicated, may hold values from 0.25 to 4
- delays: float32 [2, 4096], P(None, 'feed'), may hold values from -3 to 3
- band_phase: float32 [2, 16], replicated, may hold values from -4 to 4
- rfi_flags: int32 [512, 32], P('tm', 'chan'), may hold values 0 or 1
- grid_rows: int32 [256], replicated, may hold values from 0 to 255, each once
Outputs:
- delay_grad: float32 [2, 4096], P(None, 'feed')
- band_grad: float32 [2, 16], replicated
The draws below stay inside these ranges and needn't reach their ends.
Inputs may be any that keep to these rules, and one draw needn't show every extreme that they name: `grid_rows`: every row 0 to 255 is taken by exactly one feed position, the same for every cylinder.
All inputs are finite; a program needn't handle non-finite values. No bound on the sum of `rfi_flags` on one device may be relied on, other than what follows from the above.
Results may differ from the reference program's by a relative error of at most 0.017.
Values may be sent and summed in bfloat16 or wider, within the bound.
A program may use at most 128 MiB of HBM per device.

```python
import math
import jax
import jax.numpy as jnp
from jax import lax

CYL = 16
NSF = 256
EWB = 32
NSB = 512
POL = 2
BANDS = 16
FEEDS = 4096
TIMES = 512
CHANS = 32
TIME_GROUPS = 2
SUB_GROUPS = 32
SUB_TIMES = 8


def with_ends(array, rng, least, high):
    dims = array.shape
    spot = [jax.random.randint(jax.random.fold_in(rng, axis), (), 0, dims[axis]) for axis in range(len(dims))]
    array = array.at[tuple(spot)].set(least)
    longest = dims.index(max(dims))
    spot[longest] = (spot[longest] + 1) % dims[longest]
    return array.at[tuple(spot)].set(high)


def shard_levels(stream_key, shape, shards, least, largest):
    def one(dim, parts):
        heights = jax.random.uniform(jax.random.fold_in(jax.random.fold_in(stream_key, 6), dim), (parts,), jnp.float32, least / len(shards), largest / len(shards))
        return jnp.repeat(jnp.exp(heights), shape[dim] // parts).reshape((-1,) + (1,) * (len(shape) - dim - 1))

    level = one(*shards[0])
    for cut in shards[1:]:
        level = level * one(*cut)
    return level


def centred(rng, dims, scale, limit, shards=(), kind=jnp.bfloat16):
    drawn = jax.random.normal(rng, dims, jnp.float32) * scale
    if len(shards) > 0:
        drawn = shard_levels(rng, dims, shards, -0.22, 0.18) * drawn
    return jnp.clip(drawn, min=-limit, max=limit).astype(kind)


def setup_inputs(seed: int = 0) -> dict:
    keys = jax.random.split(jax.random.key(seed), 8)
    voltages = centred(keys[0], (2, TIMES, CHANS, POL, FEEDS), 1.0, 6.0, ((1, 2), (2, 8), (4, 32)))
    beam_refs = centred(keys[1], (2, TIME_GROUPS, SUB_GROUPS, SUB_TIMES, CHANS, POL, EWB, NSB), 0.5, 3.0, ((1, 2), (2, 32), (4, 8)))
    beam_weight = jnp.clip(jnp.exp(jax.random.uniform(keys[2], (EWB, NSB), jnp.float32, math.log(0.25), math.log(4.0))), 0.25, 4.0)
    delays = jnp.clip(jax.random.uniform(keys[3], (POL, FEEDS), jnp.float32, -3.0, 3.0) * shard_levels(keys[3], (POL, FEEDS), ((1, 32),), -0.4, 0.0), -3.0, 3.0)
    band_phase = centred(keys[4], (POL, BANDS), 1.0, 4.0, (), jnp.float32)
    rfi_flags = with_ends((jax.random.randint(keys[5], (TIMES, CHANS), 0, 8) < 1).astype(jnp.int32), jax.random.fold_in(keys[5], 1), 0, 1)
    grid_rows = jax.random.permutation(keys[6], NSF).astype(jnp.int32)
    return dict(voltages=voltages, beam_refs=beam_refs, beam_weight=beam_weight, delays=delays, band_phase=band_phase, rfi_flags=rfi_flags, grid_rows=grid_rows)


full_turn = 2.0 * math.pi

def rounded(value):
    return lax.optimization_barrier(value.astype(jnp.bfloat16)).astype(jnp.float32)

def product(form, left, right):
    return jnp.einsum(form, left, right, precision=lax.Precision.HIGHEST)

def dft_parts(grid_rows):
    cyl_index = jnp.arange(CYL, dtype=jnp.int32)
    east_index = jnp.arange(EWB, dtype=jnp.int32)
    east_angle = full_turn / EWB * (east_index[:, None] * cyl_index[None, :] % EWB).astype(jnp.float32)
    north_index = jnp.arange(NSB, dtype=jnp.int32)
    north_angle = full_turn / NSB * (north_index[:, None] * grid_rows.astype(jnp.int32)[None, :] % NSB).astype(jnp.float32)
    east_real = (jnp.cos(east_angle) / math.sqrt(EWB)).astype(jnp.bfloat16)
    east_imag = (-jnp.sin(east_angle) / math.sqrt(EWB)).astype(jnp.bfloat16)
    north_real = (jnp.cos(north_angle) / math.sqrt(NSB)).astype(jnp.bfloat16)
    north_imag = (-jnp.sin(north_angle) / math.sqrt(NSB)).astype(jnp.bfloat16)
    return (east_real, east_imag, north_real, north_imag)

def band_basis(chan_index, chans_total):
    term_index = jnp.arange(BANDS).astype(jnp.float32)
    return math.sqrt(2.0 / chans_total) * jnp.cos(math.pi * (chan_index[:, None] + 0.5) * term_index[None, :] / chans_total)

def reference(voltages, beam_refs, beam_weight, delays, band_phase, rfi_flags, grid_rows):
    tables = dft_parts(grid_rows)
    east_real = tables[0].astype(jnp.float32)
    east_imag = tables[1].astype(jnp.float32)
    north_real = tables[2].astype(jnp.float32)
    north_imag = tables[3].astype(jnp.float32)
    chan_index = jnp.arange(CHANS).astype(jnp.float32)
    frequency = 0.4 + 0.4 * (chan_index + 0.5) / CHANS
    basis = band_basis(chan_index, CHANS)
    offset = jnp.dot(band_phase, basis.T, precision=lax.Precision.HIGHEST)
    phases = full_turn * frequency[None, :, None] * delays[:, None, :] + offset[:, :, None]
    gain_real = jnp.transpose(jnp.cos(phases), (1, 0, 2))[None]
    gain_imag = jnp.transpose(-jnp.sin(phases), (1, 0, 2))[None]
    ref_field = beam_refs.reshape(2, TIMES, CHANS, POL, EWB, NSB)
    time_block = 8

    def advance(block_index, totals):
        time_start = (block_index * time_block).astype(jnp.int32)
        volt_block = lax.dynamic_slice_in_dim(voltages, time_start, time_block, 1).astype(jnp.float32)
        ref_block = lax.dynamic_slice_in_dim(ref_field, time_start, time_block, 1).astype(jnp.float32)
        flag_block = lax.dynamic_slice_in_dim(rfi_flags, time_start, time_block, 0)
        sky_real = rounded(gain_real * volt_block[0] - gain_imag * volt_block[1])
        sky_imag = rounded(gain_real * volt_block[1] + gain_imag * volt_block[0])
        grid_shape = (time_block, CHANS, POL, NSF, CYL)
        grid_real = sky_real.reshape(grid_shape)
        grid_imag = sky_imag.reshape(grid_shape)
        east_re = rounded(product('tfpnc,ec->tfpen', grid_real, east_real) - product('tfpnc,ec->tfpen', grid_imag, east_imag))
        east_im = rounded(product('tfpnc,ec->tfpen', grid_real, east_imag) + product('tfpnc,ec->tfpen', grid_imag, east_real))
        beam_re = product('tfpen,mn->tfpem', east_re, north_real) - product('tfpen,mn->tfpem', east_im, north_imag)
        beam_im = product('tfpen,mn->tfpem', east_re, north_imag) + product('tfpen,mn->tfpem', east_im, north_real)
        keep_weight = ((1 - flag_block).astype(jnp.float32) / TIMES)[:, :, None, None, None]
        resid_re = rounded(keep_weight * beam_weight * (beam_re - ref_block[0]))
        resid_im = rounded(keep_weight * beam_weight * (beam_im - ref_block[1]))
        back_re = rounded(product('tfpem,mn->tfpen', resid_re, north_real) + product('tfpem,mn->tfpen', resid_im, north_imag))
        back_im = rounded(product('tfpem,mn->tfpen', resid_im, north_real) - product('tfpem,mn->tfpen', resid_re, north_imag))
        field_re = rounded(product('tfpen,ec->tfpnc', back_re, east_real) + product('tfpen,ec->tfpnc', back_im, east_imag))
        field_im = rounded(product('tfpen,ec->tfpnc', back_im, east_real) - product('tfpen,ec->tfpnc', back_re, east_imag))
        flat_shape = (time_block, CHANS, POL, CYL * NSF)
        torque = field_re.reshape(flat_shape) * sky_imag - field_im.reshape(flat_shape) * sky_real
        delay_total = totals[0] + product('tfpj,f->pj', torque, full_turn * frequency)
        chan_total = totals[1] + lax.optimization_barrier(jnp.sum(torque, axis=(0, 3))).T
        return (delay_total, chan_total)
    start_totals = (jnp.zeros((POL, CYL * NSF), jnp.float32), jnp.zeros((POL, CHANS), jnp.float32))
    delay_total, chan_total = lax.fori_loop(0, TIMES // time_block, advance, start_totals)
    band_grad = jnp.dot(chan_total, basis, precision=lax.Precision.HIGHEST)
    return (delay_total, band_grad)
```

```python
import math

import jax
import jax.numpy as jnp
import numpy as np
from jax import lax
from jax.experimental import pallas as pl
from jax.experimental.pallas import tpu as pltpu
from jax.sharding import PartitionSpec as P

CYL = 16
NSF = 256
EWB = 32
NSB = 512
BANDS = 16
CHANS = 32
TIMES = 512
FEED = 32
CHUNKS = 4
MESH = pl.DeviceIdType.MESH
full_turn = 2.0 * math.pi
bf16 = jnp.bfloat16
f32 = jnp.float32


def constant_tables():
    e = np.arange(EWB)
    c = np.arange(CYL)
    angle = (np.float32(full_turn / EWB) * ((e[:, None] * c[None, :]) % EWB).astype(np.float32)).astype(np.float32)
    east_real = (np.cos(angle) / np.float32(math.sqrt(EWB))).astype(np.float32)
    east_imag = (-np.sin(angle) / np.float32(math.sqrt(EWB))).astype(np.float32)
    eye = np.eye(8, dtype=np.float32)
    parts = [[east_real, -east_imag], [east_imag, east_real]]
    east = np.zeros((2, 8, EWB, 2, CYL, 8), np.float32)
    for o in range(2):
        for i in range(2):
            east[o, :, :, i] = np.einsum("ec,rs->recs", parts[o][i], eye)
    east = east.reshape(2 * 8 * EWB, 2 * CYL * 8)
    m = np.arange(NSB)
    g = np.arange(NSF)
    angle = (np.float32(full_turn / NSB) * ((m[:, None] * g[None, :]) % NSB).astype(np.float32)).astype(np.float32)
    north_real = (np.cos(angle) / np.float32(math.sqrt(NSB))).astype(np.float32)
    north_imag = (-np.sin(angle) / np.float32(math.sqrt(NSB))).astype(np.float32)
    north_rows = np.concatenate([north_real.T, north_imag.T], 1)
    north_cols = np.concatenate([north_real, north_imag], 0)
    return tuple(jnp.asarray(a, bf16) for a in (east, east.T, north_rows, north_cols))


def iota(shape, dim):
    return lax.broadcasted_iota(jnp.int32, shape, dim)


def dot(a, b):
    return jnp.dot(a, b, preferred_element_type=f32)


def kernel(
    volt_hbm, refs_hbm, weight_hbm, delays_hbm, band_hbm, flags_hbm, grid_hbm,
    east_hbm, east_adj_hbm, rows_hbm, cols_hbm,
    delay_out, band_out,
    volt, refs, weight_ref, delays_ref, band_ref, flags, grid_ref, east_t, east_adj, rows_t, cols_t,
    sky, recv, north, north_adj, keep, flip, vis, gfield, acc, stack,
    piece, piece_in, total, total_in,
    load_sem, recv_sem, send_sem, sum_sem,
):
    feed = lax.axis_index("feed")
    chan = lax.axis_index("chan")
    tm = lax.axis_index("tm")
    ct = chan * 2 + tm
    fx = feed // 8
    fz = feed % 8

    def feed_peer(k):
        return ((fx + k % 4) % 4) * 8 + (fz + k // 4) % 8

    def ct_peer(k):
        return (ct + k) % 16

    barrier = pltpu.get_barrier_semaphore()

    def greet_feed(k, _):
        pl.semaphore_signal(barrier, inc=1, device_id={"feed": feed_peer(k)}, device_id_type=MESH)
        return 0

    def greet_ct(k, _):
        d = ct_peer(k)
        pl.semaphore_signal(barrier, inc=1, device_id={"chan": d // 2, "tm": d % 2}, device_id_type=MESH)
        return 0

    lax.fori_loop(1, FEED, greet_feed, 0)
    lax.fori_loop(1, 16, greet_ct, 0)

    pairs = [
        (delays_hbm, delays_ref), (band_hbm, band_ref), (volt_hbm, volt), (grid_hbm, grid_ref), (flags_hbm, flags),
        (rows_hbm, rows_t), (cols_hbm, cols_t), (weight_hbm, weight_ref), (east_hbm, east_t),
        (east_adj_hbm, east_adj), (refs_hbm, refs),
    ]
    loads = [pltpu.make_async_copy(src, dst, load_sem.at[i]) for i, (src, dst) in enumerate(pairs)]
    for copy in loads:
        copy.start()
    loads[0].wait()
    loads[1].wait()

    row = iota((8, 128), 0)
    lane = iota((8, 128), 1)
    chan_index = (chan * 4 + row // 2).astype(f32)
    freq_turn = full_turn * (0.4 + 0.4 * (chan_index + 0.5) / CHANS)
    first_pol = row % 2 == 0

    def basis_at(term):
        return math.sqrt(2.0 / CHANS) * jnp.cos(math.pi * (chan_index + 0.5) * term.astype(f32) / CHANS)

    basis = basis_at(lane % BANDS)
    coef = jnp.where(first_pol[:, :BANDS], band_ref[0:1, :], band_ref[1:2, :])
    offset = jnp.sum(coef * basis[:, :BANDS], axis=1, keepdims=True)
    phases = freq_turn * jnp.where(first_pol, delays_ref[0:1, :], delays_ref[1:2, :]) + offset
    gain_real = jnp.cos(phases)
    gain_imag = -jnp.sin(phases)
    gain_real = jnp.concatenate([gain_real, gain_real], 0)
    gain_imag = jnp.concatenate([gain_imag, gain_imag], 0)
    loads[2].wait()

    def gain_block(d, _):
        for q in range(CHUNKS):
            volt_real = volt[0, d, q].astype(f32)
            volt_imag = volt[1, d, q].astype(f32)
            sky[q, d, 0:16, :] = (gain_real * volt_real - gain_imag * volt_imag).astype(bf16)
            sky[q, d, 16:32, :] = (gain_real * volt_imag + gain_imag * volt_real).astype(bf16)
        return 0

    lax.fori_loop(0, FEED, gain_block, 0)
    pl.semaphore_wait(barrier, FEED - 1 + 15)

    def send_chunk(q, _):
        pltpu.make_async_copy(sky.at[q, feed], recv.at[q, feed], recv_sem.at[q]).start()

        def send(k, _):
            d = feed_peer(k)
            pltpu.make_async_remote_copy(
                src_ref=sky.at[q, d],
                dst_ref=recv.at[q, feed],
                send_sem=send_sem.at[q],
                recv_sem=recv_sem.at[q],
                device_id={"feed": d},
                device_id_type=MESH,
            ).start()
            return 0

        lax.fori_loop(1, FEED, send, 0)
        return 0

    lax.fori_loop(0, CHUNKS, send_chunk, 0)

    for copy in loads[3:]:
        copy.wait()
    pick_t = jnp.where(iota((NSF, NSF), 0) == grid_ref[...], 1.0, 0.0).astype(f32)
    pick = jnp.transpose(pick_t).astype(bf16)
    pick_t = pick_t.astype(bf16)
    by_n = dot(pick, rows_t[...]).astype(bf16)
    north[0:NSF, :] = by_n
    north[NSF:, 0:NSB] = -by_n[:, NSB:]
    north[NSF:, NSB:] = by_n[:, :NSB]
    by_m = dot(cols_t[...], pick_t).astype(bf16)
    north_adj[0:NSB, 0:NSF] = by_m[:NSB]
    north_adj[0:NSB, NSF:] = -by_m[NSB:]
    north_adj[NSB:, 0:NSF] = by_m[NSB:]
    north_adj[NSB:, NSF:] = by_m[:NSB]
    kept = (1 - flags[...]).astype(f32) * (1.0 / TIMES)
    kept = jnp.concatenate([kept[i // 2 : i // 2 + 1] for i in range(8)], 0)
    for t in range(8):
        at_time = jnp.where(iota((8, NSF), 1) == feed * 8 + t, kept, 0.0)
        keep[t] = jnp.broadcast_to(jnp.sum(at_time, axis=1, keepdims=True), (8, NSF))
    acc[...] = jnp.zeros_like(acc)
    stack[...] = jnp.zeros_like(stack)
    low = iota((32, 128), 1) < 64

    def chunk(q, _):
        pltpu.make_async_copy(recv.at[q], recv.at[q], recv_sem.at[q]).wait()
        for g in range(8):
            block = jnp.concatenate([recv[q, g + 8 * s] for s in range(4)], 0)
            flip[g * 128 : (g + 1) * 128, :] = jnp.transpose(block.astype(f32))
        for h in range(8):
            pair = jnp.concatenate(
                [flip[pl.ds(2 * h, 64, stride=16), :], flip[pl.ds(2 * h + 1, 64, stride=16), :]], 0
            )
            back = jnp.transpose(pair)
            u = [back[32 * s : 32 * (s + 1)] for s in range(4)]
            v = [pltpu.roll(a, 64, 1) for a in u]
            halves = [
                [jnp.where(low, u[0], v[1]), jnp.where(low, u[2], v[3])],
                [jnp.where(low, v[0], u[1]), jnp.where(low, v[2], u[3])],
            ]
            for i in range(2):
                at = (2 * h + i) * 16
                for b in range(2):
                    both = halves[i][b].astype(bf16)
                    vis[at : at + 16, b * 128 : (b + 1) * 128] = both[0:16]
                    vis[at : at + 16, NSF + b * 128 : NSF + (b + 1) * 128] = both[16:32]
        north_out = dot(vis[...], north[...]).reshape(CYL, 16, 2 * NSB)
        for t in range(2):
            one = north_out[:, 8 * t : 8 * t + 8, :].reshape(CYL * 8, 2 * NSB)
            one = jnp.concatenate([one[:, :NSB], one[:, NSB:]], 0).astype(bf16)
            beams = dot(east_t[...], one)
            first = pl.multiple_of(q * 16 + t * 8, 8)
            seen = refs[:, pl.ds(first, 8)].reshape(2 * 8 * EWB, NSB).astype(f32)
            resid = ((beams - seen).reshape(16, EWB, NSB) * weight_ref[...][None]).reshape(2 * 8 * EWB, NSB)
            adj = dot(east_adj[...], resid.astype(bf16)).astype(bf16)
            gfield[128 * t : 128 * (t + 1), 0:NSB] = adj[0:128]
            gfield[128 * t : 128 * (t + 1), NSB:] = adj[128:256]
        field = dot(gfield[...], north_adj[...])
        here = vis[...].astype(f32).reshape(CYL, 16, 2 * NSF)
        for t in range(2):
            f = field[128 * t : 128 * (t + 1)].reshape(CYL, 8, 2 * NSF)
            s = here[:, 8 * t : 8 * t + 8, :]
            torque = f[:, :, :NSF] * s[:, :, NSF:] - f[:, :, NSF:] * s[:, :, :NSF]
            acc[...] += torque * keep[2 * q + t][None]
        return 0

    lax.fori_loop(0, CHUNKS, chunk, 0)

    def over_chans(x):
        x = x + pltpu.roll(x, 4, 0)
        return x + pltpu.roll(x, 2, 0)

    wide_turn = jnp.concatenate([freq_turn, freq_turn], 1)
    for c in range(CYL):
        summed = over_chans(acc[c] * wide_turn)
        stack[c : c + 1, :] = summed[0:1]
        stack[CYL + c : CYL + c + 1, :] = summed[1:2]
    chan_sum = jnp.sum(jnp.sum(acc[...], axis=0), axis=1, keepdims=True)
    band_lanes = (lane >= 32) & (lane < 32 + BANDS)
    band = over_chans(jnp.where(band_lanes, basis * chan_sum, 0.0))
    band_high = band.astype(bf16).astype(f32)
    band = jnp.where(row < 2, band_high, jnp.where(row < 4, band - band_high, 0.0))
    for h in range(2):
        part = jnp.transpose(stack[:, 128 * h : 128 * (h + 1)]).reshape(16, 8, 128)
        piece[16 * h : 16 * (h + 1)] = (part + band[None]).astype(bf16)

    pltpu.make_async_copy(piece.at[feed], piece_in.at[feed], sum_sem.at[0]).start()

    def send_piece(k, _):
        d = feed_peer(k)
        pltpu.make_async_remote_copy(
            src_ref=piece.at[d],
            dst_ref=piece_in.at[feed],
            send_sem=sum_sem.at[1],
            recv_sem=sum_sem.at[0],
            device_id={"feed": d},
            device_id_type=MESH,
        ).start()
        return 0

    lax.fori_loop(1, FEED, send_piece, 0)
    pltpu.make_async_copy(piece_in, piece_in, sum_sem.at[0]).wait()
    total[...] = jnp.sum(piece_in[...].astype(f32), axis=0)

    pltpu.make_async_copy(total, total_in.at[ct], sum_sem.at[2]).start()

    def send_total(k, _):
        d = ct_peer(k)
        pltpu.make_async_remote_copy(
            src_ref=total,
            dst_ref=total_in.at[ct],
            send_sem=sum_sem.at[3],
            recv_sem=sum_sem.at[2],
            device_id={"chan": d // 2, "tm": d % 2},
            device_id_type=MESH,
        ).start()
        return 0

    lax.fori_loop(1, 16, send_total, 0)
    for q in range(CHUNKS):
        pltpu.make_async_copy(sky.at[q, pl.ds(0, FEED - 1)], sky.at[q, pl.ds(0, FEED - 1)], send_sem.at[q]).wait()
    some = piece.at[pl.ds(0, FEED - 1)]
    pltpu.make_async_copy(some, some, sum_sem.at[1]).wait()
    pltpu.make_async_copy(total_in, total_in, sum_sem.at[2]).wait()
    grad = jnp.sum(total_in[...], axis=0)
    own = (lane // 16) == row
    for p in range(2):
        shifted = pltpu.roll(grad, 112, 1) if p else grad
        turned = pltpu.roll(shifted, 0, 1, stride=16, stride_axis=0)
        delay_out[p : p + 1, :] = jnp.sum(jnp.where(own, turned, 0.0), axis=0, keepdims=True)
    band = pltpu.roll(grad + pltpu.roll(grad, 6, 0), 96, 1)
    band_out[...] = band[0:2, 0:BANDS]
    some = total_in.at[pl.ds(0, 15)]
    pltpu.make_async_copy(some, some, sum_sem.at[3]).wait()


def shards(voltages, beam_refs, beam_weight, delays, band_phase, rfi_flags, grid_rows):
    hbm_spec = pl.BlockSpec(memory_space=pltpu.MemorySpace.HBM)
    vmem_spec = pl.BlockSpec(memory_space=pltpu.VMEM)
    east, east_adj, rows, cols = constant_tables()
    return pl.pallas_call(
        kernel,
        out_shape=(jax.ShapeDtypeStruct((2, 128), f32), jax.ShapeDtypeStruct((2, BANDS), f32)),
        in_specs=[hbm_spec] * 11,
        out_specs=(vmem_spec, vmem_spec),
        scratch_shapes=[
            pltpu.VMEM((2, FEED, CHUNKS, 16, 128), bf16),
            pltpu.VMEM((2, 64, EWB, NSB), bf16),
            pltpu.VMEM((EWB, NSB), f32),
            pltpu.VMEM((2, 128), f32),
            pltpu.VMEM((2, BANDS), f32),
            pltpu.VMEM((4, NSF), jnp.int32),
            pltpu.VMEM((1, NSF), jnp.int32),
            pltpu.VMEM((512, 256), bf16),
            pltpu.VMEM((256, 512), bf16),
            pltpu.VMEM((256, 1024), bf16),
            pltpu.VMEM((1024, 256), bf16),
            pltpu.VMEM((CHUNKS, FEED, 32, 128), bf16),
            pltpu.VMEM((CHUNKS, FEED, 32, 128), bf16),
            pltpu.VMEM((2 * NSF, 2 * NSB), bf16),
            pltpu.VMEM((2 * NSB, 2 * NSF), bf16),
            pltpu.VMEM((8, 8, NSF), f32),
            pltpu.VMEM((8 * 128, 128), f32),
            pltpu.VMEM((256, 2 * NSF), bf16),
            pltpu.VMEM((256, 2 * NSB), bf16),
            pltpu.VMEM((CYL, 8, NSF), f32),
            pltpu.VMEM((128, NSF), f32),
            pltpu.VMEM((FEED, 8, 128), bf16),
            pltpu.VMEM((FEED, 8, 128), bf16),
            pltpu.VMEM((8, 128), f32),
            pltpu.VMEM((16, 8, 128), f32),
            pltpu.SemaphoreType.DMA((11,)),
            pltpu.SemaphoreType.DMA((CHUNKS,)),
            pltpu.SemaphoreType.DMA((CHUNKS,)),
            pltpu.SemaphoreType.DMA((4,)),
        ],
        compiler_params=pltpu.CompilerParams(
            collective_id=0, has_side_effects=True, vmem_limit_bytes=67043328
        ),
    )(
        voltages.reshape(2, FEED, CHUNKS, 16, 128),
        beam_refs.reshape(2, 64, EWB, NSB),
        beam_weight,
        delays,
        band_phase,
        rfi_flags.T,
        grid_rows.reshape(1, NSF),
        east,
        east_adj,
        rows,
        cols,
    )


def solution(mesh):
    in_specs = (
        P(None, "tm", "chan", None, "feed"),
        P(None, "tm", "feed", None, "chan", None, None, None),
        P(),
        P(None, "feed"),
        P(),
        P("tm", "chan"),
        P(),
    )
    out_specs = (P(None, "feed"), P())
    return jax.shard_map(shards, mesh=mesh, in_specs=in_specs, out_specs=out_specs, check_vma=False)
```

```python
import math

import jax
import jax.numpy as jnp
import numpy as np
from jax import lax
from jax.experimental import pallas as pl
from jax.experimental.pallas import tpu as pltpu
from jax.sharding import PartitionSpec as P

CYL = 16
NSF = 256
EWB = 32
NSB = 512
BANDS = 16
CHANS = 32
TIMES = 512
FEED = 32
CHUNKS = 4
MESH = pl.DeviceIdType.MESH
full_turn = 2.0 * math.pi
bf16 = jnp.bfloat16
f32 = jnp.float32


def constant_tables():
    e = np.arange(EWB)
    c = np.arange(CYL)
    angle = (np.float32(full_turn / EWB) * ((e[:, None] * c[None, :]) % EWB).astype(np.float32)).astype(np.float32)
    east_real = (np.cos(angle) / np.float32(math.sqrt(EWB))).astype(np.float32)
    east_imag = (-np.sin(angle) / np.float32(math.sqrt(EWB))).astype(np.float32)
    eye = np.eye(8, dtype=np.float32)
    parts = [[east_real, -east_imag], [east_imag, east_real]]
    east = np.zeros((2, 8, EWB, 2, CYL, 8), np.float32)
    for o in range(2):
        for i in range(2):
            east[o, :, :, i] = np.einsum("ec,rs->recs", parts[o][i], eye)
    east = east.reshape(2 * 8 * EWB, 2 * CYL * 8)
    m = np.arange(NSB)
    g = np.arange(NSF)
    angle = (np.float32(full_turn / NSB) * ((m[:, None] * g[None, :]) % NSB).astype(np.float32)).astype(np.float32)
    north_real = (np.cos(angle) / np.float32(math.sqrt(NSB))).astype(np.float32)
    north_imag = (-np.sin(angle) / np.float32(math.sqrt(NSB))).astype(np.float32)
    north_rows = np.concatenate([north_real.T, north_imag.T], 1)
    north_cols = np.concatenate([north_real, north_imag], 0)
    return tuple(jnp.asarray(a, bf16) for a in (east, east.T, north_rows, north_cols))


def iota(shape, dim):
    return lax.broadcasted_iota(jnp.int32, shape, dim)


def dot(a, b):
    return jnp.dot(a, b, preferred_element_type=f32)


def spread(size):
    return [(size // 2 + (i + 1) // 2 * (-1) ** i) % size for i in range(size)]


OFFSETS = [(dx, dz) for dx in spread(4) for dz in spread(8)][:-1]


def kernel(
    volt_hbm, refs_hbm, weight_hbm, delays_hbm, band_hbm, flags_hbm, grid_hbm,
    east_hbm, east_adj_hbm, rows_hbm, cols_hbm,
    out,
    volt, refs, weight_ref, delays_ref, band_ref, flags, grid_ref, east_t, east_adj, rows_t, cols_t,
    sky, recv, north, north_adj, keep, flip, vis, gfield, acc, stack,
    piece, piece_in, total, total_in,
    load_sem, recv_sem, send_sem, sum_sem,
):
    feed = lax.axis_index("feed")
    chan = lax.axis_index("chan")
    tm = lax.axis_index("tm")
    ct = chan * 2 + tm
    fx = feed // 8
    fz = feed % 8

    def feed_peer(offset):
        return ((fx + offset[0]) % 4) * 8 + (fz + offset[1]) % 8

    def ct_peer(k):
        dy = 4 + (k // 2 + 1) // 2 * (1 - 2 * (k // 2 % 2))
        return (chan + dy) % 8, (tm + 1 - k % 2) % 2

    barrier = pltpu.get_barrier_semaphore()

    for offset in OFFSETS:
        pl.semaphore_signal(barrier, inc=1, device_id={"feed": feed_peer(offset)}, device_id_type=MESH)

    def greet_ct(k, _):
        y, core = ct_peer(k)
        pl.semaphore_signal(barrier, inc=1, device_id={"chan": y, "tm": core}, device_id_type=MESH)
        return 0

    lax.fori_loop(0, 15, greet_ct, 0)

    pairs = [
        (delays_hbm, delays_ref), (band_hbm, band_ref), (volt_hbm, volt), (grid_hbm, grid_ref), (flags_hbm, flags),
        (rows_hbm, rows_t), (cols_hbm, cols_t), (weight_hbm, weight_ref), (east_hbm, east_t),
        (east_adj_hbm, east_adj), (refs_hbm, refs),
    ]
    loads = [pltpu.make_async_copy(src, dst, load_sem.at[i]) for i, (src, dst) in enumerate(pairs)]
    for copy in loads:
        copy.start()
    loads[0].wait()
    loads[1].wait()

    row = iota((8, 128), 0)
    lane = iota((8, 128), 1)
    chan_index = (chan * 4 + row // 2).astype(f32)
    freq_turn = full_turn * (0.4 + 0.4 * (chan_index + 0.5) / CHANS)
    first_pol = row % 2 == 0

    def basis_at(term):
        return math.sqrt(2.0 / CHANS) * jnp.cos(math.pi * (chan_index + 0.5) * term.astype(f32) / CHANS)

    basis = basis_at(lane % BANDS)
    coef = jnp.where(first_pol[:, :BANDS], band_ref[0:1, :], band_ref[1:2, :])
    offset = jnp.sum(coef * basis[:, :BANDS], axis=1, keepdims=True)
    phases = freq_turn * jnp.where(first_pol, delays_ref[0:1, :], delays_ref[1:2, :]) + offset
    gain_real = jnp.cos(phases)
    gain_imag = -jnp.sin(phases)
    gain_real = jnp.concatenate([gain_real, gain_real], 0)
    gain_imag = jnp.concatenate([gain_imag, gain_imag], 0)
    loads[2].wait()

    def gain_block(d, _):
        for q in range(CHUNKS):
            volt_real = volt[0, d, q].astype(f32)
            volt_imag = volt[1, d, q].astype(f32)
            sky[q, d, 0:16, :] = (gain_real * volt_real - gain_imag * volt_imag).astype(bf16)
            sky[q, d, 16:32, :] = (gain_real * volt_imag + gain_imag * volt_real).astype(bf16)
        return 0

    lax.fori_loop(0, FEED, gain_block, 0)
    pl.semaphore_wait(barrier, FEED - 1 + 15)

    def send_chunk(q, _):
        pltpu.make_async_copy(sky.at[q, feed], recv.at[q, feed], recv_sem.at[q]).start()

        for offset in OFFSETS:
            d = feed_peer(offset)
            pltpu.make_async_remote_copy(
                src_ref=sky.at[q, d],
                dst_ref=recv.at[q, feed],
                send_sem=send_sem.at[q],
                recv_sem=recv_sem.at[q],
                device_id={"feed": d},
                device_id_type=MESH,
            ).start()
        return 0

    lax.fori_loop(0, CHUNKS, send_chunk, 0)

    for copy in loads[3:]:
        copy.wait()
    pick_t = jnp.where(iota((NSF, NSF), 0) == grid_ref[...], 1.0, 0.0).astype(f32)
    pick = jnp.transpose(pick_t).astype(bf16)
    pick_t = pick_t.astype(bf16)
    by_n = dot(pick, rows_t[...]).astype(bf16)
    north[0:NSF, :] = by_n
    north[NSF:, 0:NSB] = -by_n[:, NSB:]
    north[NSF:, NSB:] = by_n[:, :NSB]
    by_m = dot(cols_t[...], pick_t).astype(bf16)
    north_adj[0:NSB, 0:NSF] = by_m[:NSB]
    north_adj[0:NSB, NSF:] = -by_m[NSB:]
    north_adj[NSB:, 0:NSF] = by_m[NSB:]
    north_adj[NSB:, NSF:] = by_m[:NSB]
    kept = (1 - flags[...]).astype(f32) * (1.0 / TIMES)
    kept = jnp.concatenate([kept[i // 2 : i // 2 + 1] for i in range(8)], 0)
    for t in range(8):
        at_time = jnp.where(iota((8, NSF), 1) == feed * 8 + t, kept, 0.0)
        keep[t] = jnp.broadcast_to(jnp.sum(at_time, axis=1, keepdims=True), (8, NSF))
    acc[...] = jnp.zeros_like(acc)
    stack[...] = jnp.zeros_like(stack)
    low = iota((32, 128), 1) < 64

    def chunk(q, _):
        pltpu.make_async_copy(recv.at[q], recv.at[q], recv_sem.at[q]).wait()
        for g in range(8):
            block = jnp.concatenate([recv[q, g + 8 * s] for s in range(4)], 0)
            flip[g * 128 : (g + 1) * 128, :] = jnp.transpose(block.astype(f32))
        for h in range(8):
            pair = jnp.concatenate(
                [flip[pl.ds(2 * h, 64, stride=16), :], flip[pl.ds(2 * h + 1, 64, stride=16), :]], 0
            )
            back = jnp.transpose(pair)
            u = [back[32 * s : 32 * (s + 1)] for s in range(4)]
            v = [pltpu.roll(a, 64, 1) for a in u]
            halves = [
                [jnp.where(low, u[0], v[1]), jnp.where(low, u[2], v[3])],
                [jnp.where(low, v[0], u[1]), jnp.where(low, v[2], u[3])],
            ]
            for i in range(2):
                at = (2 * h + i) * 16
                for b in range(2):
                    both = halves[i][b].astype(bf16)
                    vis[at : at + 16, b * 128 : (b + 1) * 128] = both[0:16]
                    vis[at : at + 16, NSF + b * 128 : NSF + (b + 1) * 128] = both[16:32]
        north_out = dot(vis[...], north[...]).reshape(CYL, 16, 2 * NSB)
        for t in range(2):
            one = north_out[:, 8 * t : 8 * t + 8, :].reshape(CYL * 8, 2 * NSB)
            one = jnp.concatenate([one[:, :NSB], one[:, NSB:]], 0).astype(bf16)
            beams = dot(east_t[...], one)
            first = pl.multiple_of(q * 16 + t * 8, 8)
            seen = refs[:, pl.ds(first, 8)].reshape(2 * 8 * EWB, NSB).astype(f32)
            resid = ((beams - seen).reshape(16, EWB, NSB) * weight_ref[...][None]).reshape(2 * 8 * EWB, NSB)
            adj = dot(east_adj[...], resid.astype(bf16)).astype(bf16)
            gfield[128 * t : 128 * (t + 1), 0:NSB] = adj[0:128]
            gfield[128 * t : 128 * (t + 1), NSB:] = adj[128:256]
        field = dot(gfield[...], north_adj[...])
        here = vis[...].astype(f32).reshape(CYL, 16, 2 * NSF)
        for t in range(2):
            f = field[128 * t : 128 * (t + 1)].reshape(CYL, 8, 2 * NSF)
            s = here[:, 8 * t : 8 * t + 8, :]
            torque = f[:, :, :NSF] * s[:, :, NSF:] - f[:, :, NSF:] * s[:, :, :NSF]
            acc[...] += torque * keep[2 * q + t][None]
        return 0

    lax.fori_loop(0, CHUNKS, chunk, 0)

    def over_chans(x):
        x = x + pltpu.roll(x, 4, 0)
        return x + pltpu.roll(x, 2, 0)

    wide_turn = jnp.concatenate([freq_turn, freq_turn], 1)
    for c in range(CYL):
        summed = over_chans(acc[c] * wide_turn)
        stack[c : c + 1, :] = summed[0:1]
        stack[CYL + c : CYL + c + 1, :] = summed[1:2]
    chan_sum = jnp.sum(jnp.sum(acc[...], axis=0), axis=1, keepdims=True)
    band_lanes = (lane >= 32) & (lane < 32 + BANDS)
    band = over_chans(jnp.where(band_lanes, basis * chan_sum, 0.0))
    band_high = band.astype(bf16).astype(f32)
    band = jnp.where(row % 4 < 2, band_high, band - band_high)
    for h in range(2):
        flip[128 * h : 128 * (h + 1), :] = jnp.transpose(stack[:, 128 * h : 128 * (h + 1)])
    packed = flip[pl.ds(0, 128, stride=2), :] + pltpu.roll(flip[pl.ds(1, 128, stride=2), :], 64, 1)
    packed = (packed.reshape(16, 8, 128) + band[None]).reshape(FEED, 4, 128)
    piece[...] = packed.astype(bf16)

    pltpu.make_async_copy(piece.at[feed], piece_in.at[feed], sum_sem.at[0]).start()

    for offset in OFFSETS:
        d = feed_peer(offset)
        pltpu.make_async_remote_copy(
            src_ref=piece.at[d],
            dst_ref=piece_in.at[feed],
            send_sem=sum_sem.at[1],
            recv_sem=sum_sem.at[0],
            device_id={"feed": d},
            device_id_type=MESH,
        ).start()
    pltpu.make_async_copy(piece_in, piece_in, sum_sem.at[0]).wait()
    total[...] = jnp.sum(piece_in[...].astype(f32), axis=0)

    pltpu.make_async_copy(total, total_in.at[ct], sum_sem.at[2]).start()

    def send_total(k, _):
        y, core = ct_peer(k)
        pltpu.make_async_remote_copy(
            src_ref=total,
            dst_ref=total_in.at[ct],
            send_sem=sum_sem.at[3],
            recv_sem=sum_sem.at[2],
            device_id={"chan": y, "tm": core},
            device_id_type=MESH,
        ).start()
        return 0

    lax.fori_loop(0, 15, send_total, 0)
    for q in range(CHUNKS):
        pltpu.make_async_copy(sky.at[q, pl.ds(0, FEED - 1)], sky.at[q, pl.ds(0, FEED - 1)], send_sem.at[q]).wait()
    some = piece.at[pl.ds(0, FEED - 1)]
    pltpu.make_async_copy(some, some, sum_sem.at[1]).wait()
    pltpu.make_async_copy(total_in, total_in, sum_sem.at[2]).wait()
    grad = jnp.sum(total_in[...], axis=0)
    pair = iota((4, 128), 0)
    slot = iota((4, 128), 1) // 16
    for p in range(2):
        delay = jnp.zeros((4, 128), f32)
        for h in range(2):
            for r in range(4):
                turned = pltpu.roll(grad, (32 * r - 48 * h - 16 * p) % 128, 1)
                delay = jnp.where((pair == r) & (slot == 2 * r + h), turned, delay)
        out[p : p + 1, :] = jnp.sum(delay, axis=0, keepdims=True)
    band = pltpu.roll(grad, 96, 1)
    out[2:4, :] = band[0:2] + band[2:4]
    some = total_in.at[pl.ds(0, 15)]
    pltpu.make_async_copy(some, some, sum_sem.at[3]).wait()


def shards(voltages, beam_refs, beam_weight, delays, band_phase, rfi_flags, grid_rows):
    hbm_spec = pl.BlockSpec(memory_space=pltpu.MemorySpace.HBM)
    east, east_adj, rows, cols = constant_tables()
    grads = pl.pallas_call(
        kernel,
        out_shape=jax.ShapeDtypeStruct((4, 128), f32),
        in_specs=[hbm_spec] * 11,
        out_specs=pl.BlockSpec(memory_space=pltpu.VMEM),
        scratch_shapes=[
            pltpu.VMEM((2, FEED, CHUNKS, 16, 128), bf16),
            pltpu.VMEM((2, 64, EWB, NSB), bf16),
            pltpu.VMEM((EWB, NSB), f32),
            pltpu.VMEM((2, 128), f32),
            pltpu.VMEM((2, BANDS), f32),
            pltpu.VMEM((4, NSF), jnp.int32),
            pltpu.VMEM((1, NSF), jnp.int32),
            pltpu.VMEM((512, 256), bf16),
            pltpu.VMEM((256, 512), bf16),
            pltpu.VMEM((256, 1024), bf16),
            pltpu.VMEM((1024, 256), bf16),
            pltpu.VMEM((CHUNKS, FEED, 32, 128), bf16),
            pltpu.VMEM((CHUNKS, FEED, 32, 128), bf16),
            pltpu.VMEM((2 * NSF, 2 * NSB), bf16),
            pltpu.VMEM((2 * NSB, 2 * NSF), bf16),
            pltpu.VMEM((8, 8, NSF), f32),
            pltpu.VMEM((8 * 128, 128), f32),
            pltpu.VMEM((256, 2 * NSF), bf16),
            pltpu.VMEM((256, 2 * NSB), bf16),
            pltpu.VMEM((CYL, 8, NSF), f32),
            pltpu.VMEM((128, NSF), f32),
            pltpu.VMEM((FEED, 4, 128), bf16),
            pltpu.VMEM((FEED, 4, 128), bf16),
            pltpu.VMEM((4, 128), f32),
            pltpu.VMEM((16, 4, 128), f32),
            pltpu.SemaphoreType.DMA((11,)),
            pltpu.SemaphoreType.DMA((CHUNKS,)),
            pltpu.SemaphoreType.DMA((CHUNKS,)),
            pltpu.SemaphoreType.DMA((4,)),
        ],
        compiler_params=pltpu.CompilerParams(
            collective_id=0, has_side_effects=True, vmem_limit_bytes=56000000
        ),
    )(*[pltpu.with_memory_space_constraint(a, pltpu.MemorySpace.HBM) for a in (
        voltages.reshape(2, FEED, CHUNKS, 16, 128),
        beam_refs.reshape(2, 64, EWB, NSB),
        beam_weight,
        delays,
        band_phase,
        rfi_flags.T,
        grid_rows.reshape(1, NSF),
        east,
        east_adj,
        rows,
        cols,
        )])
    return grads[0:2], grads[2:4, 0:BANDS]


def solution(mesh):
    in_specs = (
        P(None, "tm", "chan", None, "feed"),
        P(None, "tm", "feed", None, "chan", None, None, None),
        P(),
        P(None, "feed"),
        P(),
        P("tm", "chan"),
        P(),
    )
    out_specs = (P(None, "feed"), P())
    return jax.shard_map(shards, mesh=mesh, in_specs=in_specs, out_specs=out_specs, check_vma=False)
```

```python
import math

import jax
import jax.numpy as jnp
import numpy as np
from jax import lax
from jax.experimental import pallas as pl
from jax.experimental.pallas import tpu as pltpu
from jax.sharding import PartitionSpec as P

CYL = 16
NSF = 256
EWB = 32
NSB = 512
BANDS = 16
CHANS = 32
TIMES = 512
FEED = 32
CHUNKS = 4
MESH = pl.DeviceIdType.MESH
full_turn = 2.0 * math.pi
bf16 = jnp.bfloat16
f32 = jnp.float32


def constant_tables():
    e = np.arange(EWB)
    c = np.arange(CYL)
    angle = (np.float32(full_turn / EWB) * ((e[:, None] * c[None, :]) % EWB).astype(np.float32)).astype(np.float32)
    east_real = (np.cos(angle) / np.float32(math.sqrt(EWB))).astype(np.float32)
    east_imag = (-np.sin(angle) / np.float32(math.sqrt(EWB))).astype(np.float32)
    eye = np.eye(8, dtype=np.float32)
    parts = [[east_real, -east_imag], [east_imag, east_real]]
    east = np.zeros((2, 8, EWB, 2, CYL, 8), np.float32)
    for o in range(2):
        for i in range(2):
            east[o, :, :, i] = np.einsum("ec,rs->recs", parts[o][i], eye)
    east = east.reshape(2 * 8 * EWB, 2 * CYL * 8)
    m = np.arange(NSB)
    g = np.arange(NSF)
    angle = (np.float32(full_turn / NSB) * ((m[:, None] * g[None, :]) % NSB).astype(np.float32)).astype(np.float32)
    north_real = (np.cos(angle) / np.float32(math.sqrt(NSB))).astype(np.float32)
    north_imag = (-np.sin(angle) / np.float32(math.sqrt(NSB))).astype(np.float32)
    north_rows = np.concatenate([north_real.T, north_imag.T], 1)
    north_cols = np.concatenate([north_real, north_imag], 0)
    return tuple(jnp.asarray(a, bf16) for a in (east, east.T, north_rows, north_cols))


def iota(shape, dim):
    return lax.broadcasted_iota(jnp.int32, shape, dim)


def dot(a, b):
    return jnp.dot(a, b, preferred_element_type=f32)


def spread(size):
    return [(size // 2 + (i + 1) // 2 * (-1) ** i) % size for i in range(size)]


OFFSETS = [(dx, dz) for dx in spread(4) for dz in spread(8)][:-1]
MESSAGES = ((0, 4), (4, 7), (7, 8))


def kernel(
    volt_hbm, refs_hbm, weight_hbm, delays_hbm, band_hbm, flags_hbm, grid_hbm,
    east_hbm, east_adj_hbm, rows_hbm, cols_hbm,
    out,
    volt, refs, weight_ref, delays_ref, band_ref, flags, grid_ref, east_t, east_adj, rows_t, cols_t,
    sky, recv, north, north_adj, keep, flip, vis, gfield, acc, stack,
    piece, piece_in, total, total_in,
    load_sem, recv_sem, send_sem, sum_sem,
):
    feed = lax.axis_index("feed")
    chan = lax.axis_index("chan")
    tm = lax.axis_index("tm")
    ct = chan * 2 + tm
    fx = feed // 8
    fz = feed % 8

    def feed_peer(offset):
        return ((fx + offset[0]) % 4) * 8 + (fz + offset[1]) % 8

    def ct_peer(k):
        dy = 4 + (k // 2 + 1) // 2 * (1 - 2 * (k // 2 % 2))
        return (chan + dy) % 8, (tm + 1 - k % 2) % 2

    barrier = pltpu.get_barrier_semaphore()

    for offset in OFFSETS:
        pl.semaphore_signal(barrier, inc=1, device_id={"feed": feed_peer(offset)}, device_id_type=MESH)

    def greet_ct(k, _):
        y, core = ct_peer(k)
        pl.semaphore_signal(barrier, inc=1, device_id={"chan": y, "tm": core}, device_id_type=MESH)
        return 0

    lax.fori_loop(0, 15, greet_ct, 0)

    pairs = [
        (delays_hbm, delays_ref), (band_hbm, band_ref), (volt_hbm, volt), (grid_hbm, grid_ref), (flags_hbm, flags),
        (rows_hbm, rows_t), (cols_hbm, cols_t), (weight_hbm, weight_ref), (east_hbm, east_t),
        (east_adj_hbm, east_adj), (refs_hbm, refs),
    ]
    loads = [pltpu.make_async_copy(src, dst, load_sem.at[i]) for i, (src, dst) in enumerate(pairs)]
    for copy in loads:
        copy.start()
    loads[0].wait()
    loads[1].wait()

    row = iota((8, 128), 0)
    lane = iota((8, 128), 1)
    chan_index = (chan * 4 + row // 2).astype(f32)
    freq_turn = full_turn * (0.4 + 0.4 * (chan_index + 0.5) / CHANS)
    first_pol = row % 2 == 0

    def basis_at(term):
        return math.sqrt(2.0 / CHANS) * jnp.cos(math.pi * (chan_index + 0.5) * term.astype(f32) / CHANS)

    basis = basis_at(lane % BANDS)
    coef = jnp.where(first_pol[:, :BANDS], band_ref[0:1, :], band_ref[1:2, :])
    offset = jnp.sum(coef * basis[:, :BANDS], axis=1, keepdims=True)
    phases = freq_turn * jnp.where(first_pol, delays_ref[0:1, :], delays_ref[1:2, :]) + offset
    gain_real = jnp.cos(phases)
    gain_imag = -jnp.sin(phases)
    gain_real = jnp.concatenate([gain_real, gain_real], 0)
    gain_imag = jnp.concatenate([gain_imag, gain_imag], 0)
    loads[2].wait()

    def gain_block(d, _):
        for q in range(CHUNKS):
            volt_real = volt[0, d, q].astype(f32)
            volt_imag = volt[1, d, q].astype(f32)
            sky_real = gain_real * volt_real - gain_imag * volt_imag
            sky_imag = gain_real * volt_imag + gain_imag * volt_real
            for t in range(2):
                sky[d, 2 * q + t, 0] = sky_real[8 * t : 8 * t + 8].astype(bf16)
                sky[d, 2 * q + t, 1] = sky_imag[8 * t : 8 * t + 8].astype(bf16)
        return 0

    lax.fori_loop(0, FEED, gain_block, 0)
    pl.semaphore_wait(barrier, FEED - 1 + 15)

    for m, (first, last) in enumerate(MESSAGES):
        pltpu.make_async_copy(sky.at[feed, first:last], recv.at[feed, first:last], recv_sem.at[m]).start()
        for offset in OFFSETS:
            d = feed_peer(offset)
            pltpu.make_async_remote_copy(
                src_ref=sky.at[d, first:last],
                dst_ref=recv.at[feed, first:last],
                send_sem=send_sem.at[m],
                recv_sem=recv_sem.at[m],
                device_id={"feed": d},
                device_id_type=MESH,
            ).start()

    for copy in loads[3:]:
        copy.wait()
    pick_t = jnp.where(iota((NSF, NSF), 0) == grid_ref[...], 1.0, 0.0).astype(f32)
    pick = jnp.transpose(pick_t).astype(bf16)
    pick_t = pick_t.astype(bf16)
    by_n = dot(pick, rows_t[...]).astype(bf16)
    north[0:NSF, :] = by_n
    north[NSF:, 0:NSB] = -by_n[:, NSB:]
    north[NSF:, NSB:] = by_n[:, :NSB]
    by_m = dot(cols_t[...], pick_t).astype(bf16)
    north_adj[0:NSB, 0:NSF] = by_m[:NSB]
    north_adj[0:NSB, NSF:] = -by_m[NSB:]
    north_adj[NSB:, 0:NSF] = by_m[NSB:]
    north_adj[NSB:, NSF:] = by_m[:NSB]
    kept = (1 - flags[...]).astype(f32) * (1.0 / TIMES)
    kept = jnp.concatenate([kept[i // 2 : i // 2 + 1] for i in range(8)], 0)
    for t in range(8):
        at_time = jnp.where(iota((8, NSF), 1) == feed * 8 + t, kept, 0.0)
        keep[t] = jnp.broadcast_to(jnp.sum(at_time, axis=1, keepdims=True), (8, NSF))
    acc[...] = jnp.zeros_like(acc)
    stack[...] = jnp.zeros_like(stack)
    low = iota((32, 128), 1) < 64

    def arrived(time):
        for m, (first, last) in enumerate(MESSAGES):

            @pl.when(time == first)
            def _():
                part = recv.at[:, first:last]
                pltpu.make_async_copy(part, part, recv_sem.at[m]).wait()

    def place(at, rows, both):
        for b in range(2):
            vis[at : at + rows, b * 128 : (b + 1) * 128] = both[b][0:rows].astype(bf16)
            vis[at : at + rows, NSF + b * 128 : NSF + (b + 1) * 128] = both[b][rows : 2 * rows].astype(bf16)

    def gather_pair(time):
        for g in range(8):
            block = [recv[g + 8 * s, pl.ds(time, 2)].astype(f32).reshape(32, 128) for s in range(4)]
            flip[g * 128 : (g + 1) * 128, :] = jnp.transpose(jnp.concatenate(block, 0))
        for h in range(8):
            pair = [flip[pl.ds(2 * h + i, 64, stride=16), :] for i in range(2)]
            back = jnp.transpose(jnp.concatenate(pair, 0))
            u = [back[32 * s : 32 * (s + 1)] for s in range(4)]
            v = [pltpu.roll(a, 64, 1) for a in u]
            halves = [
                [jnp.where(low, u[0], v[1]), jnp.where(low, u[2], v[3])],
                [jnp.where(low, v[0], u[1]), jnp.where(low, v[2], u[3])],
            ]
            for i in range(2):
                both = [jnp.concatenate([a[0:8], a[16:24], a[8:16], a[24:32]], 0) for a in halves[i]]
                place((2 * h + i) * 16, 16, both)

    quarter = iota((16, 128), 1) // 32

    def gather_one(time):
        for g in range(4):
            block = [recv[4 * s + g, time].astype(f32).reshape(16, 128) for s in range(8)]
            flip[g * 128 : (g + 1) * 128, :] = jnp.transpose(jnp.concatenate(block, 0))
        for h in range(4):
            four = [flip[pl.ds(4 * h + i, 32, stride=16), :] for i in range(4)]
            back = jnp.transpose(jnp.concatenate(four, 0))
            u = [back[16 * s : 16 * (s + 1)] for s in range(8)]
            for i in range(4):
                both = []
                for b in range(2):
                    half = jnp.zeros((16, 128), f32)
                    for j in range(4):
                        shift = 32 * (j - i) % 128
                        moved = pltpu.roll(u[4 * b + j], shift, 1) if shift else u[4 * b + j]
                        half = jnp.where(quarter == j, moved, half)
                    both.append(half)
                place((4 * h + i) * 8, 8, both)

    def gradient(time, times):
        rows = CYL * 8 * times
        north_out = dot(vis[0:rows], north[...]).reshape(CYL, 8 * times, 2 * NSB)
        for t in range(times):
            one = north_out[:, 8 * t : 8 * t + 8, :].reshape(CYL * 8, 2 * NSB)
            one = jnp.concatenate([one[:, :NSB], one[:, NSB:]], 0).astype(bf16)
            beams = dot(east_t[...], one)
            first = pl.multiple_of((time + t) * 8, 8)
            seen = refs[:, pl.ds(first, 8)].reshape(2 * 8 * EWB, NSB).astype(f32)
            resid = ((beams - seen).reshape(16, EWB, NSB) * weight_ref[...][None]).reshape(2 * 8 * EWB, NSB)
            adj = dot(east_adj[...], resid.astype(bf16)).astype(bf16)
            gfield[128 * t : 128 * (t + 1), 0:NSB] = adj[0:128]
            gfield[128 * t : 128 * (t + 1), NSB:] = adj[128:256]
        field = dot(gfield[0:rows], north_adj[...])
        here = vis[0:rows].astype(f32).reshape(CYL, 8 * times, 2 * NSF)
        for t in range(times):
            f = field[128 * t : 128 * (t + 1)].reshape(CYL, 8, 2 * NSF)
            s = here[:, 8 * t : 8 * t + 8, :]
            torque = f[:, :, :NSF] * s[:, :, NSF:] - f[:, :, NSF:] * s[:, :, :NSF]
            acc[...] += torque * keep[time + t][None]

    def pair_step(i, _):
        time = 2 * i
        arrived(time)
        gather_pair(time)
        gradient(time, 2)
        return 0

    def one_step(time, _):
        arrived(time)
        gather_one(time)
        gradient(time, 1)
        return 0

    lax.fori_loop(0, 3, pair_step, 0)
    lax.fori_loop(6, 8, one_step, 0)

    def over_chans(x):
        x = x + pltpu.roll(x, 4, 0)
        return x + pltpu.roll(x, 2, 0)

    wide_turn = jnp.concatenate([freq_turn, freq_turn], 1)
    for c in range(CYL):
        summed = over_chans(acc[c] * wide_turn)
        stack[c : c + 1, :] = summed[0:1]
        stack[CYL + c : CYL + c + 1, :] = summed[1:2]
    chan_sum = jnp.sum(jnp.sum(acc[...], axis=0), axis=1, keepdims=True)
    band_lanes = (lane >= 32) & (lane < 32 + BANDS)
    band = over_chans(jnp.where(band_lanes, basis * chan_sum, 0.0))
    band_high = band.astype(bf16).astype(f32)
    band = jnp.where(row % 4 < 2, band_high, band - band_high)
    for h in range(2):
        flip[128 * h : 128 * (h + 1), :] = jnp.transpose(stack[:, 128 * h : 128 * (h + 1)])
    packed = flip[pl.ds(0, 128, stride=2), :] + pltpu.roll(flip[pl.ds(1, 128, stride=2), :], 64, 1)
    packed = (packed.reshape(16, 8, 128) + band[None]).reshape(FEED, 4, 128)
    piece[...] = packed.astype(bf16)

    pltpu.make_async_copy(piece.at[feed], piece_in.at[feed], sum_sem.at[0]).start()

    for offset in OFFSETS:
        d = feed_peer(offset)
        pltpu.make_async_remote_copy(
            src_ref=piece.at[d],
            dst_ref=piece_in.at[feed],
            send_sem=sum_sem.at[1],
            recv_sem=sum_sem.at[0],
            device_id={"feed": d},
            device_id_type=MESH,
        ).start()
    pltpu.make_async_copy(piece_in, piece_in, sum_sem.at[0]).wait()
    total[...] = jnp.sum(piece_in[...].astype(f32), axis=0)

    pltpu.make_async_copy(total, total_in.at[ct], sum_sem.at[2]).start()

    def send_total(k, _):
        y, core = ct_peer(k)
        pltpu.make_async_remote_copy(
            src_ref=total,
            dst_ref=total_in.at[ct],
            send_sem=sum_sem.at[3],
            recv_sem=sum_sem.at[2],
            device_id={"chan": y, "tm": core},
            device_id_type=MESH,
        ).start()
        return 0

    lax.fori_loop(0, 15, send_total, 0)
    for m, (first, last) in enumerate(MESSAGES):
        some = sky.at[0 : FEED - 1, first:last]
        pltpu.make_async_copy(some, some, send_sem.at[m]).wait()
    some = piece.at[pl.ds(0, FEED - 1)]
    pltpu.make_async_copy(some, some, sum_sem.at[1]).wait()
    pltpu.make_async_copy(total_in, total_in, sum_sem.at[2]).wait()
    grad = jnp.sum(total_in[...], axis=0)
    pair = iota((4, 128), 0)
    slot = iota((4, 128), 1) // 16
    for p in range(2):
        delay = jnp.zeros((4, 128), f32)
        for h in range(2):
            for r in range(4):
                turned = pltpu.roll(grad, (32 * r - 48 * h - 16 * p) % 128, 1)
                delay = jnp.where((pair == r) & (slot == 2 * r + h), turned, delay)
        out[p : p + 1, :] = jnp.sum(delay, axis=0, keepdims=True)
    band = pltpu.roll(grad, 96, 1)
    out[2:4, :] = band[0:2] + band[2:4]
    some = total_in.at[pl.ds(0, 15)]
    pltpu.make_async_copy(some, some, sum_sem.at[3]).wait()


def shards(voltages, beam_refs, beam_weight, delays, band_phase, rfi_flags, grid_rows):
    hbm_spec = pl.BlockSpec(memory_space=pltpu.MemorySpace.HBM)
    east, east_adj, rows, cols = constant_tables()
    grads = pl.pallas_call(
        kernel,
        out_shape=jax.ShapeDtypeStruct((4, 128), f32),
        in_specs=[hbm_spec] * 11,
        out_specs=pl.BlockSpec(memory_space=pltpu.VMEM),
        scratch_shapes=[
            pltpu.VMEM((2, FEED, CHUNKS, 16, 128), bf16),
            pltpu.VMEM((2, 64, EWB, NSB), bf16),
            pltpu.VMEM((EWB, NSB), f32),
            pltpu.VMEM((2, 128), f32),
            pltpu.VMEM((2, BANDS), f32),
            pltpu.VMEM((4, NSF), jnp.int32),
            pltpu.VMEM((1, NSF), jnp.int32),
            pltpu.VMEM((512, 256), bf16),
            pltpu.VMEM((256, 512), bf16),
            pltpu.VMEM((256, 1024), bf16),
            pltpu.VMEM((1024, 256), bf16),
            pltpu.VMEM((FEED, 8, 2, 8, 128), bf16),
            pltpu.VMEM((FEED, 8, 2, 8, 128), bf16),
            pltpu.VMEM((2 * NSF, 2 * NSB), bf16),
            pltpu.VMEM((2 * NSB, 2 * NSF), bf16),
            pltpu.VMEM((8, 8, NSF), f32),
            pltpu.VMEM((8 * 128, 128), f32),
            pltpu.VMEM((256, 2 * NSF), bf16),
            pltpu.VMEM((256, 2 * NSB), bf16),
            pltpu.VMEM((CYL, 8, NSF), f32),
            pltpu.VMEM((128, NSF), f32),
            pltpu.VMEM((FEED, 4, 128), bf16),
            pltpu.VMEM((FEED, 4, 128), bf16),
            pltpu.VMEM((4, 128), f32),
            pltpu.VMEM((16, 4, 128), f32),
            pltpu.SemaphoreType.DMA((11,)),
            pltpu.SemaphoreType.DMA((len(MESSAGES),)),
            pltpu.SemaphoreType.DMA((len(MESSAGES),)),
            pltpu.SemaphoreType.DMA((4,)),
        ],
        compiler_params=pltpu.CompilerParams(
            collective_id=0, has_side_effects=True, vmem_limit_bytes=56000000
        ),
    )(*[pltpu.with_memory_space_constraint(a, pltpu.MemorySpace.HBM) for a in (
        voltages.reshape(2, FEED, CHUNKS, 16, 128),
        beam_refs.reshape(2, 64, EWB, NSB),
        beam_weight,
        delays,
        band_phase,
        rfi_flags.T,
        grid_rows.reshape(1, NSF),
        east,
        east_adj,
        rows,
        cols,
        )])
    return grads[0:2], grads[2:4, 0:BANDS]


def solution(mesh):
    in_specs = (
        P(None, "tm", "chan", None, "feed"),
        P(None, "tm", "feed", None, "chan", None, None, None),
        P(),
        P(None, "feed"),
        P(),
        P("tm", "chan"),
        P(),
    )
    out_specs = (P(None, "feed"), P())
    return jax.shard_map(shards, mesh=mesh, in_specs=in_specs, out_specs=out_specs, check_vma=False)
```
